256 devices in a mesh: freq: 64 (over y, x_hi, z), tm: 4 (over x_lo, core).
Axes of the slice: x: 4 (x_hi: 2, x_lo: 2; x = x_hi * 2 + x_lo), y: 4, z: 8, core: 2. Of those that a mesh axis runs over, the one named last changes fastest.
Arguments:
- voltages: bfloat16 [512, 2, 1024, 1024], P(None, None, 'freq', 'tm'), may hold values from -6 to 6
- pattern: int32 [4, 2], replicated, may hold values from 0 to 3, as said below
- owner_map: int32 [4], replicated, may hold values from 0 to 3, each once
- channel_mask: int32 [512], P('freq'), may hold values from 0 to 1, as said below
- running_mean: float32 [4, 128, 128], P('tm'), may hold values from 2 to 32
- running_var: float32 [4, 128, 128], P('tm'), may hold values from 16 to 256
Outputs:
- stokes: float32 [4, 512, 4, 2, 128, 128], P('tm', 'freq')
- flag_weights: float32 [4, 512, 128, 128], P('tm', 'freq')
The draws below stay inside these ranges and needn't reach their ends.
Inputs may be any that keep to these rules, and one draw needn't show every extreme that they name: `pattern`: each row is a pair of antenna block numbers, the first not above the second; no pair appears twice; the pair (0, 3) is always among them. `channel_mask`: at least one channel is usable.
All inputs are finite; a program needn't handle non-finite values.
Results may differ from the reference program's by a relative error of at most 0.0003.
Values may be sent and summed in bfloat16 or wider, within the bound.
No kernel may reach another device: no remote copies, remote signals or barrier semaphores. Data moves between devices by JAX's collectives and lax.ppermute only.
A program may use at most 128 MiB of HBM per device.

```python
import math
import jax
import jax.numpy as jnp
import numpy as np
from jax import lax

BLOCK = 128
NBLOCKS = 4
SIGNALS = 1024
CH_DEV = 8
CHANNELS = 512
SAMPLES = 1024
TILES = 4


def draw_pattern(key, part):
    corners = np.array([[row_id, col_id] for row_id in range(NBLOCKS) for col_id in range(row_id, NBLOCKS)], dtype=np.int32)
    anchor = NBLOCKS - 1
    others = jnp.asarray(np.array([index for index in range(corners.shape[0]) if index != anchor], dtype=np.int32))
    picked = others[jax.random.permutation(jax.random.fold_in(key, 11), corners.shape[0] - 1)[:TILES - 1]]
    chosen = jnp.concatenate([jnp.array([anchor], dtype=jnp.int32), picked.astype(jnp.int32)])
    chosen = chosen[jax.random.permutation(jax.random.fold_in(key, 23), TILES)]
    return jnp.asarray(corners, dtype=jnp.int32)[chosen]


def draw_channel_mask(key, part):
    levels = jax.random.randint(jax.random.fold_in(key, 31), (CHANNELS,), 0, 8)
    forced = jax.random.randint(jax.random.fold_in(key, 37), (), 0, CHANNELS)
    places = jnp.arange(CHANNELS, dtype=jnp.int32)
    return jnp.where((levels < 7) | (places == forced), 1, 0).astype(jnp.int32)


def steps_of(rng, dims, shards, smallest, top_value):
    factor_of, own = 1.0, jax.random.fold_in(rng, 6)
    for dim, blocks in shards:
        heights = jnp.exp(jax.random.uniform(jax.random.fold_in(own, dim), (blocks,), jnp.float32, smallest / len(shards), top_value / len(shards)))
        factor_of = factor_of * jnp.repeat(heights, dims[dim] // blocks).reshape([-1 if axis == dim else 1 for axis in range(len(dims))])
    return factor_of


def scatter_about(key, shape, deviation, most, split=(), kind=jnp.bfloat16):
    drawn = jax.random.normal(key, shape, jnp.float32) * deviation
    if len(split) > 0:
        drawn = steps_of(key, shape, split, -0.22, 0.18) * drawn
    return jnp.clip(drawn, min=-most, max=most).astype(kind)


def setup_inputs(seed: int = 0) -> dict:
    keys = jax.random.split(jax.random.key(seed), 7)
    return {
        "voltages": scatter_about(keys[0], (CHANNELS, 2, SIGNALS, SAMPLES), 1.0, 6.0, ((2, 64), (3, 4))),
        "pattern": draw_pattern(jax.random.fold_in(keys[6], 71), 0),
        "owner_map": jax.random.permutation(keys[2], TILES).astype(jnp.int32),
        "channel_mask": draw_channel_mask(jax.random.fold_in(keys[6], 71), 0),
        "running_mean": jnp.clip(jnp.exp(math.log(32.0) - 2.7725887 * jax.random.uniform(keys[4], (TILES, BLOCK, BLOCK), jnp.float32) ** steps_of(keys[4], (TILES, BLOCK, BLOCK), ((0, 4),), -0.2, 0.2)), 2.0, 32.0),
        "running_var": jnp.clip(jnp.exp(math.log(256.0) - 2.7725887 * jax.random.uniform(keys[5], (TILES, BLOCK, BLOCK), jnp.float32) ** steps_of(keys[5], (TILES, BLOCK, BLOCK), ((0, 4),), -0.2, 0.2)), 16.0, 256.0),
    }


mixing = 0.25

def correlate(row_side, col_side):
    real_part = jnp.einsum('...rit,...rjt->...ij', row_side, col_side, precision=lax.Precision.HIGHEST)
    rotated = jnp.stack([row_side[..., 1, :, :], -row_side[..., 0, :, :]], axis=-3)
    imag_part = jnp.einsum('...rit,...rjt->...ij', rotated, col_side, precision=lax.Precision.HIGHEST)
    return jnp.stack([real_part, imag_part], axis=-3)

def reference(voltages, pattern, owner_map, channel_mask, running_mean, running_var):
    tile_width = 2 * BLOCK
    row_blocks = pattern[owner_map, 0].astype(jnp.int32)
    col_blocks = pattern[owner_map, 1].astype(jnp.int32)
    grouped = voltages.reshape((CHANNELS // CH_DEV, CH_DEV) + voltages.shape[1:])

    def per_group(channel_group):
        pieces = []
        for number in range(TILES):
            row_side = lax.dynamic_slice_in_dim(channel_group, row_blocks[number] * tile_width, tile_width, 2).astype(jnp.float32)
            col_side = lax.dynamic_slice_in_dim(channel_group, col_blocks[number] * tile_width, tile_width, 2).astype(jnp.float32)
            pieces.append(correlate(row_side, col_side))
        return jnp.stack(pieces)
    blocks = lax.map(per_group, grouped)
    summed = jnp.moveaxis(blocks, 0, 1).reshape((TILES, CHANNELS, 2, tile_width, tile_width))
    visible = summed * (1.0 / math.sqrt(SAMPLES))
    pol_xx = visible[..., :BLOCK, :BLOCK]
    pol_xy = visible[..., :BLOCK, BLOCK:]
    pol_yx = visible[..., BLOCK:, :BLOCK]
    pol_yy = visible[..., BLOCK:, BLOCK:]
    stokes_i = pol_xx + pol_yy
    stokes_q = pol_xx - pol_yy
    stokes_u = pol_xy + pol_yx
    cross_diff = pol_xy - pol_yx
    stokes_v = jnp.stack([cross_diff[:, :, 1], -cross_diff[:, :, 0]], axis=2)
    stokes = jnp.stack([stokes_i, stokes_q, stokes_u, stokes_v], axis=2)
    intensity = stokes_i[:, :, 0] ** 2 + stokes_i[:, :, 1] ** 2
    live_mask = channel_mask.astype(jnp.float32)[None, :, None, None]
    live_count = jnp.sum(channel_mask.astype(jnp.float32))
    first_sum = lax.optimization_barrier(jnp.sum(live_mask * intensity, axis=1)) / live_count
    second_sum = lax.optimization_barrier(jnp.sum(live_mask * intensity * intensity, axis=1)) / live_count
    blended_mean = (1.0 - mixing) * running_mean + mixing * first_sum
    spread = (1.0 - mixing) * running_var + mixing * (second_sum - first_sum * first_sum) + mixing * (1.0 - mixing) * (first_sum - running_mean) ** 2
    flag_weights = live_mask / (1.0 + (intensity - blended_mean[:, None]) ** 2 / spread[:, None])
    return (stokes, flag_weights)
```

```python
import math

import jax
import jax.numpy as jnp
from jax import lax
from jax.experimental import pallas as pl
from jax.experimental.pallas import tpu as pltpu
from jax.sharding import PartitionSpec as P

BLOCK = 128
BOTH = ("freq", "tm")
mixing = 0.25


def nt(left, right):
    return lax.dot_general(
        left, right, (((1,), (1,)), ((), ())), preferred_element_type=jnp.float32
    )


def correlate_kernel(scale, rows_id, cols_id, live_ref, row_ref, col_ref, stokes_ref, moment_ref):
    channel = pl.program_id(1)
    pieces = row_ref.shape[2]
    width = row_ref.shape[1] * row_ref.shape[5]
    depth = row_ref.shape[6]

    def side(ref, piece, part):
        return ref[0, :, piece, 0, part].reshape(width, depth)

    real = jnp.zeros((width, width), jnp.float32)
    imag = jnp.zeros((width, width), jnp.float32)
    for piece in range(pieces):
        row_re, row_im = side(row_ref, piece, 0), side(row_ref, piece, 1)
        col_re, col_im = side(col_ref, piece, 0), side(col_ref, piece, 1)
        real += nt(row_re, col_re) + nt(row_im, col_im)
        imag += nt(row_im, col_re) - nt(row_re, col_im)
    real = real * scale
    imag = imag * scale
    low, high = slice(0, BLOCK), slice(BLOCK, 2 * BLOCK)
    i_re = real[low, low] + real[high, high]
    i_im = imag[low, low] + imag[high, high]
    stokes_ref[0, 0, 0, 0] = i_re
    stokes_ref[0, 0, 0, 1] = i_im
    stokes_ref[0, 0, 1, 0] = real[low, low] - real[high, high]
    stokes_ref[0, 0, 1, 1] = imag[low, low] - imag[high, high]
    stokes_ref[0, 0, 2, 0] = real[low, high] + real[high, low]
    stokes_ref[0, 0, 2, 1] = imag[low, high] + imag[high, low]
    stokes_ref[0, 0, 3, 0] = imag[low, high] - imag[high, low]
    stokes_ref[0, 0, 3, 1] = real[high, low] - real[low, high]
    power = i_re * i_re + i_im * i_im
    masked = power * live_ref[channel].astype(jnp.float32)

    @pl.when(channel == 0)
    def _():
        moment_ref[0, 0] = masked
        moment_ref[0, 1] = masked * power

    @pl.when(channel > 0)
    def _():
        moment_ref[0, 0] += masked
        moment_ref[0, 1] += masked * power


def correlate(turned, rows_id, cols_id, live, samples):
    blocks, per_block, pieces, channels, _, signals, depth = turned.shape
    slots = rows_id.shape[0]
    block = (1, per_block, pieces, 1, 2, signals, depth)
    return pl.pallas_call(
        lambda *refs: correlate_kernel(1.0 / math.sqrt(samples), *refs),
        grid_spec=pltpu.PrefetchScalarGridSpec(
            num_scalar_prefetch=3,
            grid=(slots, channels),
            in_specs=[
                pl.BlockSpec(block, lambda k, c, rows, cols, live: (rows[k], 0, 0, c, 0, 0, 0)),
                pl.BlockSpec(block, lambda k, c, rows, cols, live: (cols[k], 0, 0, c, 0, 0, 0)),
            ],
            out_specs=[
                pl.BlockSpec((1, 1, 4, 2, BLOCK, BLOCK), lambda k, c, *_: (k, c, 0, 0, 0, 0)),
                pl.BlockSpec((1, 2, BLOCK, BLOCK), lambda k, c, *_: (k, 0, 0, 0)),
            ],
        ),
        out_shape=[
            jax.ShapeDtypeStruct((slots, channels, 4, 2, BLOCK, BLOCK), jnp.float32),
            jax.ShapeDtypeStruct((slots, 2, BLOCK, BLOCK), jnp.float32),
        ],
        compiler_params=pltpu.CompilerParams(vmem_limit_bytes=32 << 20),
        cost_estimate=pl.CostEstimate(
            flops=slots * channels * 8 * (2 * BLOCK) ** 2 * samples,
            bytes_accessed=slots * channels * (4 << 20),
            transcendentals=0,
        ),
        name="correlate",
    )(rows_id, cols_id, live, turned, turned)


def local(voltages, pattern, owner_map, channel_mask, running_mean, running_var):
    freq_count, tm_count = lax.axis_size("freq"), lax.axis_size("tm")
    blocks = 4
    everyone = freq_count * tm_count
    total, _, signals, depth = voltages.shape
    mine = total // everyone
    ordered = pattern[owner_map]
    rows_id, cols_id = ordered[:, 0], ordered[:, 1]
    turned = lax.all_to_all(voltages, BOTH, split_axis=0, concat_axis=0, tiled=True)
    turned = turned.reshape(
        blocks, freq_count // blocks, tm_count, mine, 2, signals, depth
    )
    live = lax.dynamic_slice_in_dim(channel_mask, lax.axis_index("tm") * mine, mine, 0)
    stokes, moments = correlate(turned, rows_id, cols_id, live, depth * tm_count)
    slots = rows_id.shape[0]
    stokes = lax.all_to_all(
        stokes.reshape((slots * mine,) + stokes.shape[2:]), "tm", split_axis=0, concat_axis=0, tiled=True
    )
    stokes = stokes.reshape((1,) + stokes.shape)
    count_row = jnp.broadcast_to(
        jnp.sum(live.astype(jnp.float32)), (slots, freq_count, 1, BLOCK)
    )
    sent = moments.reshape(slots, 2, freq_count, BLOCK // freq_count, BLOCK)
    sent = sent.transpose(2, 0, 1, 3, 4).reshape(everyone, -1, BLOCK)
    rows = sent.shape[1]
    sent = jnp.concatenate([sent, count_row.reshape(everyone, 1, BLOCK)], axis=1)
    summed = jnp.sum(
        lax.all_to_all(sent, BOTH, split_axis=0, concat_axis=0, tiled=True).reshape(
            everyone, rows + 1, BLOCK
        ),
        axis=0,
    )
    planes = summed[:rows] / summed[rows:]
    planes = lax.all_to_all(
        jnp.broadcast_to(planes, (freq_count,) + planes.shape), "freq", 0, 0, tiled=True
    )
    planes = planes.reshape(freq_count, 2, BLOCK // freq_count, BLOCK).transpose(1, 0, 2, 3)
    first, second = planes.reshape(2, 1, BLOCK, BLOCK)
    intensity = stokes[:, :, 0, 0] ** 2 + stokes[:, :, 0, 1] ** 2
    live_mask = channel_mask.astype(jnp.float32)[None, :, None, None]
    blended = (1.0 - mixing) * running_mean + mixing * first
    spread = (
        (1.0 - mixing) * running_var
        + mixing * (second - first * first)
        + mixing * (1.0 - mixing) * (first - running_mean) ** 2
    )
    weights = live_mask / (1.0 + (intensity - blended[:, None]) ** 2 / spread[:, None])
    return (stokes, weights)


def solution(mesh):
    return jax.shard_map(
        local,
        mesh=mesh,
        in_specs=(
            P(None, None, "freq", "tm"),
            P(),
            P(),
            P("freq"),
            P("tm", None, None),
            P("tm", None, None),
        ),
        out_specs=(P("tm", "freq", None, None, None, None), P("tm", "freq", None, None)),
        check_vma=False,
    )
```

```python
import math

import jax
import jax.numpy as jnp
from jax import lax
from jax.experimental import pallas as pl
from jax.experimental.pallas import tpu as pltpu
from jax.sharding import Mesh, PartitionSpec as P

BLOCK = 128
mixing = 0.25

FREQ = ("y", "xh", "z")
TM = ("xl", "core")
ALL = FREQ + TM
SHAPE = (4, 2, 8, 2, 2)
SLOTS = 4
FREQS = 64
MINE = 2
BAND = BLOCK // 4
PIECE = (MINE, 4, 2, BLOCK, BLOCK)


def nt(left, right):
    return lax.dot_general(
        left, right, (((1,), (1,)), ((), ())), preferred_element_type=jnp.float32
    )


def correlate_kernel(scale, ids, turned_ref, *refs):
    outs, moment_ref, stage, sems = refs[:SLOTS], refs[SLOTS], refs[SLOTS + 1], refs[SLOTS + 2]
    channel, step = pl.program_id(0), pl.program_id(1)
    _, per_block, pieces, _, _, signals, depth = turned_ref.shape
    width = per_block * signals

    def side(block, part):
        return [
            turned_ref[block, :, piece, 0, part].reshape(width, depth) for piece in range(pieces)
        ]

    row, col = ids[step], ids[SLOTS + step]
    row_re, row_im = side(row, 0), side(row, 1)
    columns = jnp.concatenate(side(col, 0) + side(col, 1), axis=1)
    rows = jnp.concatenate(
        [
            jnp.concatenate(row_re + row_im, axis=1),
            jnp.concatenate(row_im + [-part for part in row_re], axis=1),
        ],
        axis=0,
    )
    both = nt(rows, columns) * scale
    low, high = slice(0, BLOCK), slice(BLOCK, 2 * BLOCK)
    real, imag = both[:width], both[width:]
    i_re = real[low, low] + real[high, high]
    i_im = imag[low, low] + imag[high, high]
    stage[step, channel, 0, 0] = i_re
    stage[step, channel, 0, 1] = i_im
    stage[step, channel, 1, 0] = real[low, low] - real[high, high]
    stage[step, channel, 1, 1] = imag[low, low] - imag[high, high]
    stage[step, channel, 2, 0] = real[low, high] + real[high, low]
    stage[step, channel, 2, 1] = imag[low, high] + imag[high, low]
    stage[step, channel, 3, 0] = imag[low, high] - imag[high, low]
    stage[step, channel, 3, 1] = real[high, low] - real[low, high]

    def copy(number, index):
        return pltpu.make_async_copy(
            stage.at[number, index], outs[number].at[index], sems.at[number, index]
        )

    for number in range(SLOTS):
        for index in range(MINE):

            @pl.when((step == number) & (channel == index))
            def _():
                copy(number, index).start()

    power = i_re * i_re + i_im * i_im
    masked = power * ids[3 * SLOTS + channel].astype(jnp.float32)
    slot = ids[2 * SLOTS + step]
    for order, plane in enumerate((masked, masked * power)):

        @pl.when(channel == 0)
        def _():
            moment_ref[slot, order] = plane

        @pl.when(channel > 0)
        def _():
            moment_ref[slot, order] += plane

    @pl.when((step == SLOTS - 1) & (channel == MINE - 1))
    def _():
        for number in range(SLOTS):
            for index in range(MINE):
                copy(number, index).wait()


def correlate(ids, turned, samples):
    blocks, per_block, pieces, channels, _, signals, depth = turned.shape
    block = (blocks, per_block, pieces, 1, 2, signals, depth)
    moments = (SLOTS, 2, BLOCK, BLOCK)
    return pl.pallas_call(
        lambda *refs: correlate_kernel(1.0 / math.sqrt(samples), *refs),
        grid_spec=pltpu.PrefetchScalarGridSpec(
            num_scalar_prefetch=1,
            grid=(channels, SLOTS),
            in_specs=[pl.BlockSpec(block, lambda c, k, ids: (0, 0, 0, c, 0, 0, 0))],
            out_specs=[pl.BlockSpec(memory_space=pl.ANY)] * SLOTS
            + [pl.BlockSpec(moments, lambda c, k, ids: (0,) * 4)],
            scratch_shapes=[
                pltpu.VMEM((SLOTS,) + PIECE, jnp.float32),
                pltpu.SemaphoreType.DMA((SLOTS, MINE)),
            ],
        ),
        out_shape=[jax.ShapeDtypeStruct(PIECE, jnp.float32)] * SLOTS
        + [jax.ShapeDtypeStruct(moments, jnp.float32)],
        compiler_params=pltpu.CompilerParams(vmem_limit_bytes=32 << 20),
        cost_estimate=pl.CostEstimate(
            flops=SLOTS * channels * 8 * (2 * BLOCK) ** 2 * samples,
            bytes_accessed=13 << 20,
            transcendentals=0,
        ),
        name="correlate",
    )(ids, turned)


def finish_kernel(ids, mask, count_ref, planes_ref, mean_ref, var_ref, *refs):
    pieces, (stokes_ref, weight_ref, sems) = refs[:SLOTS], refs[SLOTS:]
    copies = []
    for number in range(SLOTS):
        first_row = MINE * ids[2 * SLOTS + number]
        placed = pltpu.make_async_copy(
            pieces[number], stokes_ref.at[0, pl.ds(first_row, MINE)], sems.at[number]
        )
        placed.start()
        copies.append(placed)
    count = jnp.sum(count_ref[...], axis=0, keepdims=True)
    for band in range(BLOCK // BAND):
        rows = slice(band * BAND, (band + 1) * BAND)
        first = planes_ref[0, rows] / count
        second = planes_ref[1, rows] / count
        mean = mean_ref[0, rows]
        blended = (1.0 - mixing) * mean + mixing * first
        spread = (
            (1.0 - mixing) * var_ref[0, rows]
            + mixing * (second - first * first)
            + mixing * (1.0 - mixing) * (first - mean) ** 2
        )
        for number in range(SLOTS):
            for index in range(MINE):
                place = MINE * ids[2 * SLOTS + number] + index
                live = mask[place].astype(jnp.float32)
                i_re, i_im = pieces[number][index, 0, 0, rows], pieces[number][index, 0, 1, rows]
                off = i_re * i_re + i_im * i_im - blended
                weight_ref[0, place, rows] = live / (1.0 + off * off / spread)
    for placed in copies:
        placed.wait()


def finish(ids, mask, count, planes, mean, var, pieces):
    whole = pl.BlockSpec(memory_space=pltpu.VMEM)
    scalars = pl.BlockSpec(memory_space=pltpu.SMEM)
    return pl.pallas_call(
        finish_kernel,
        in_specs=[scalars] * 2 + [whole] * (4 + SLOTS),
        out_specs=[pl.BlockSpec(memory_space=pltpu.HBM), whole],
        out_shape=[
            jax.ShapeDtypeStruct((1, MINE * SLOTS, 4, 2, BLOCK, BLOCK), jnp.float32),
            jax.ShapeDtypeStruct((1, MINE * SLOTS, BLOCK, BLOCK), jnp.float32),
        ],
        scratch_shapes=[pltpu.SemaphoreType.DMA((SLOTS,))],
        compiler_params=pltpu.CompilerParams(vmem_limit_bytes=32 << 20),
        cost_estimate=pl.CostEstimate(flops=1 << 21, bytes_accessed=8 << 20, transcendentals=0),
        name="finish",
    )(ids, mask, count, planes, mean, var, *pieces)


def swap(value, names, size, step):
    return lax.ppermute(value, names, [(i, i ^ step) for i in range(size)])


def exchange(value, names):
    return lax.all_to_all(value, names, split_axis=0, concat_axis=0, tiled=True)


def local(voltages, pattern, owner_map, channel_mask, running_mean, running_var):
    total, _, signals, depth = voltages.shape
    own = lax.axis_index(TM)
    slots = jnp.arange(SLOTS, dtype=jnp.int32)
    order = own ^ slots
    tiles = jnp.sum(jnp.where(order[:, None] == slots[None], owner_map[None], 0), axis=1)
    corners = jnp.sum(jnp.where((tiles[:, None] == slots[None])[..., None], pattern[None], 0), axis=1)
    lives = jnp.sum(
        jnp.where(own == slots[:, None], channel_mask.reshape(SLOTS, MINE), 0), axis=0
    )
    ids = jnp.concatenate([corners[:, 0], corners[:, 1], order, lives]).astype(jnp.int32)

    turned = exchange(voltages, ALL)
    turned = turned.reshape(4, FREQS // 4, SLOTS, MINE, 2, signals, depth)
    *pieces, moments = correlate(ids, turned, depth * SLOTS)

    pieces = [pieces[0]] + [swap(pieces[step], TM, SLOTS, step) for step in range(1, SLOTS)]

    rows = BLOCK // FREQS
    part = moments.reshape(SLOTS, 2, FREQS, rows, BLOCK).transpose(2, 0, 1, 3, 4)
    part = jnp.sum(exchange(part.reshape(FREQS * SLOTS, 2 * rows, BLOCK), ALL), axis=0)
    live = jnp.full((1, BLOCK), jnp.sum(channel_mask).astype(jnp.float32))
    part = jnp.concatenate([part, live], axis=0)
    parts = exchange(jnp.broadcast_to(part, (FREQS,) + part.shape), FREQ)
    planes = parts[:, : 2 * rows].reshape(FREQS, 2, rows, BLOCK).transpose(1, 0, 2, 3)
    planes = planes.reshape(2, BLOCK, BLOCK)
    count = parts[:, 2 * rows]
    return tuple(
        finish(ids, channel_mask, count, planes, running_mean, running_var, pieces)
    )


def solution(mesh):
    torus = Mesh(mesh.devices.reshape(SHAPE), ALL)
    return jax.shard_map(
        local,
        mesh=torus,
        in_specs=(
            P(None, None, FREQ, TM),
            P(),
            P(),
            P(FREQ),
            P(TM, None, None),
            P(TM, None, None),
        ),
        out_specs=(P(TM, FREQ, None, None, None, None), P(TM, FREQ, None, None)),
        check_vma=False,
    )
```

```python
import math

import jax
import jax.numpy as jnp
from jax import lax
from jax.experimental import pallas as pl
from jax.experimental.pallas import tpu as pltpu
from jax.sharding import Mesh, PartitionSpec as P

BLOCK = 128
mixing = 0.25

FREQ = ("y", "xh", "z")
TM = ("xl", "core")
ALL = FREQ + TM
SHAPE = (4, 2, 8, 2, 2)
SLOTS = 4
FREQS = 64
MINE = 2
BAND = BLOCK // 4
PLANES = (4, 2, BLOCK, BLOCK)
PARTS = ((0, 0, 2), (1, 0, 2), (2, 0, 2), (3, 0, 1), (3, 1, 1))


def nt(left, right):
    return lax.dot_general(
        left, right, (((1,), (1,)), ((), ())), preferred_element_type=jnp.float32
    )


def correlate_kernel(scale, ids, turned_ref, *refs):
    outs, moment_ref = refs[: len(PARTS)], refs[len(PARTS)]
    loaded, stage, load_sems, sems = refs[len(PARTS) + 1 :]
    blocks, per_block, pieces, _, _, signals, depth = turned_ref.shape
    width = per_block * signals

    def load(channel, block):
        return pltpu.make_async_copy(
            turned_ref.at[block, :, :, channel], loaded.at[channel, block], load_sems.at[channel, block]
        )

    def copy(number, channel):
        for out, (step, first, many) in zip(outs, PARTS):
            if step == number and first <= channel < first + many:
                return pltpu.make_async_copy(
                    stage.at[number, channel], out.at[channel - first], sems.at[number, channel]
                )

    def side(channel, block, part):
        return [
            loaded[channel, block, :, piece, part].reshape(width, depth) for piece in range(pieces)
        ]

    for channel in range(MINE):
        for block in range(blocks):
            load(channel, block).start()
    low, high = slice(0, BLOCK), slice(BLOCK, 2 * BLOCK)
    for channel in range(MINE):
        live = ids[3 * SLOTS + channel].astype(jnp.float32)
        for block in range(blocks):
            load(channel, block).wait()
        for number in range(SLOTS):
            row, col, slot = ids[number], ids[SLOTS + number], ids[2 * SLOTS + number]
            row_re, row_im = side(channel, row, 0), side(channel, row, 1)
            columns = jnp.concatenate(side(channel, col, 0) + side(channel, col, 1), axis=1)
            real = nt(jnp.concatenate(row_re + row_im, axis=1), columns) * scale
            minus_re = [-part for part in row_re]
            imag = nt(jnp.concatenate(row_im + minus_re, axis=1), columns) * scale
            i_re = real[low, low] + real[high, high]
            i_im = imag[low, low] + imag[high, high]
            stage[number, channel, 0, 0] = i_re
            stage[number, channel, 0, 1] = i_im
            stage[number, channel, 1, 0] = real[low, low] - real[high, high]
            stage[number, channel, 1, 1] = imag[low, low] - imag[high, high]
            stage[number, channel, 2, 0] = real[low, high] + real[high, low]
            stage[number, channel, 2, 1] = imag[low, high] + imag[high, low]
            stage[number, channel, 3, 0] = imag[low, high] - imag[high, low]
            stage[number, channel, 3, 1] = real[high, low] - real[low, high]
            copy(number, channel).start()
            power = i_re * i_re + i_im * i_im
            masked = power * live
            for order, plane in enumerate((masked, masked * power)):
                if channel > 0:
                    plane = plane + moment_ref[slot, order]
                moment_ref[slot, order] = plane
    for channel in range(MINE):
        for number in range(SLOTS):
            copy(number, channel).wait()


def correlate(ids, turned, samples):
    blocks, per_block, pieces, channels, _, signals, depth = turned.shape
    anywhere = pl.BlockSpec(memory_space=pl.ANY)
    return pl.pallas_call(
        lambda *refs: correlate_kernel(1.0 / math.sqrt(samples), *refs),
        in_specs=[pl.BlockSpec(memory_space=pltpu.SMEM), anywhere],
        out_specs=[anywhere] * len(PARTS) + [pl.BlockSpec(memory_space=pltpu.VMEM)],
        scratch_shapes=[
            pltpu.VMEM((channels, blocks, per_block, pieces, 2, signals, depth), turned.dtype),
            pltpu.VMEM((SLOTS, channels) + PLANES, jnp.float32),
            pltpu.SemaphoreType.DMA((channels, blocks)),
            pltpu.SemaphoreType.DMA((SLOTS, channels)),
        ],
        out_shape=[jax.ShapeDtypeStruct((many,) + PLANES, jnp.float32) for _, _, many in PARTS]
        + [jax.ShapeDtypeStruct((SLOTS, 2, BLOCK, BLOCK), jnp.float32)],
        compiler_params=pltpu.CompilerParams(vmem_limit_bytes=16 << 20),
        cost_estimate=pl.CostEstimate(
            flops=SLOTS * channels * 8 * (2 * BLOCK) ** 2 * samples,
            bytes_accessed=13 << 20,
            transcendentals=0,
        ),
        name="correlate",
    )(ids, turned)


def spread_kernel(mask, bands_ref, _, held_ref, passed_ref, part_ref, sem):
    passed = pltpu.make_async_copy(held_ref, passed_ref, sem)
    passed.start()
    total = jnp.sum(bands_ref[...], axis=0)
    live = mask[0]
    for index in range(1, mask.shape[0]):
        live = live + mask[index]
    rows = total.shape[0]
    row = jnp.full((1, BLOCK), live.astype(jnp.float32))
    for receiver in range(part_ref.shape[0]):
        part_ref[receiver, :rows] = total
        part_ref[receiver, rows:] = row
    passed.wait()


def spread_sums(mask, bands, earlier, held):
    whole = pl.BlockSpec(memory_space=pltpu.VMEM)
    anywhere = pl.BlockSpec(memory_space=pl.ANY)
    return pl.pallas_call(
        spread_kernel,
        in_specs=[pl.BlockSpec(memory_space=pltpu.SMEM), whole, whole, anywhere],
        out_specs=[whole] * 2,
        out_shape=[
            jax.ShapeDtypeStruct(held.shape, jnp.float32),
            jax.ShapeDtypeStruct((FREQS, bands.shape[1] + 1, BLOCK), jnp.float32),
        ],
        scratch_shapes=[pltpu.SemaphoreType.DMA],
        cost_estimate=pl.CostEstimate(flops=1 << 18, bytes_accessed=1 << 20, transcendentals=0),
        name="spread_sums",
    )(mask, bands, earlier, held)


def finish_kernel(parts, ids, mask, count_ref, planes_ref, mean_ref, var_ref, *refs):
    pieces, (stokes_ref, weight_ref, loaded, stage, sems) = refs[: len(parts)], refs[-5:]
    loads, copies = [], []
    for index, (_, _, many) in enumerate(parts):
        loads.append(
            pltpu.make_async_copy(pieces[index], loaded.at[index, pl.ds(0, many)], sems.at[index, 0])
        )
        loads[-1].start()
    count = jnp.sum(count_ref[...], axis=0, keepdims=True)
    bands = []
    for band in range(BLOCK // BAND):
        rows = slice(band * BAND, (band + 1) * BAND)
        first = planes_ref[0, rows] / count
        second = planes_ref[1, rows] / count
        mean = mean_ref[0, rows]
        blended = (1.0 - mixing) * mean + mixing * first
        spread = (
            (1.0 - mixing) * var_ref[0, rows]
            + mixing * (second - first * first)
            + mixing * (1.0 - mixing) * (first - mean) ** 2
        )
        bands.append((rows, blended, spread))
    for index, (step, start, many) in enumerate(parts):
        place = MINE * ids[2 * SLOTS + step] + start
        span, held = pl.ds(place, many), pl.ds(0, many)
        loads[index].wait()
        copies.append(
            pltpu.make_async_copy(
                loaded.at[index, held], stokes_ref.at[0, span], sems.at[index, 1]
            )
        )
        copies[-1].start()
        for channel in range(many):
            live = mask[place + channel].astype(jnp.float32)
            for rows, blended, spread in bands:
                i_re, i_im = loaded[index, channel, 0, 0, rows], loaded[index, channel, 0, 1, rows]
                off = i_re * i_re + i_im * i_im - blended
                stage[index, channel, rows] = live / (1.0 + off * off / spread)
        copies.append(
            pltpu.make_async_copy(stage.at[index, held], weight_ref.at[0, span], sems.at[index, 2])
        )
        copies[-1].start()
    for copy in copies:
        copy.wait()


def finish(parts, cost, ids, mask, ready, pieces, outs):
    whole = pl.BlockSpec(memory_space=pltpu.VMEM)
    scalars = pl.BlockSpec(memory_space=pltpu.SMEM)
    placed = pl.BlockSpec(memory_space=pltpu.HBM)
    anywhere = pl.BlockSpec(memory_space=pl.ANY)
    count = len(parts)
    return pl.pallas_call(
        lambda *refs: finish_kernel(parts, *refs),
        in_specs=[scalars] * 2
        + [whole] * 4
        + [placed if step == 0 else anywhere for step, _, _ in parts]
        + [placed] * len(outs),
        out_specs=[placed] * 2,
        out_shape=[
            jax.ShapeDtypeStruct((1, MINE * SLOTS) + PLANES, jnp.float32),
            jax.ShapeDtypeStruct((1, MINE * SLOTS, BLOCK, BLOCK), jnp.float32),
        ],
        input_output_aliases={6 + count + index: index for index in range(len(outs))},
        scratch_shapes=[
            pltpu.VMEM((count, MINE) + PLANES, jnp.float32),
            pltpu.VMEM((count, MINE, BLOCK, BLOCK), jnp.float32),
            pltpu.SemaphoreType.DMA((count, 3)),
        ],
        compiler_params=pltpu.CompilerParams(vmem_limit_bytes=16 << 20),
        cost_estimate=pl.CostEstimate(
            flops=cost, bytes_accessed=count << 21, transcendentals=0
        ),
        name=f"finish_{count}",
    )(ids, mask, *ready, *pieces, *outs)


def swap(value, names, size, step):
    return lax.ppermute(value, names, [(i, i ^ step) for i in range(size)])


def exchange(value, names):
    return lax.all_to_all(value, names, split_axis=0, concat_axis=0, tiled=True)


def local(voltages, pattern, owner_map, channel_mask, running_mean, running_var):
    total, _, signals, depth = voltages.shape
    own = lax.axis_index(TM)
    slots = jnp.arange(SLOTS, dtype=jnp.int32)
    order = own ^ slots
    tiles = jnp.sum(jnp.where(order[:, None] == slots[None], owner_map[None], 0), axis=1)
    corners = jnp.sum(jnp.where((tiles[:, None] == slots[None])[..., None], pattern[None], 0), axis=1)
    lives = jnp.sum(
        jnp.where(own == slots[:, None], channel_mask.reshape(SLOTS, MINE), 0), axis=0
    )
    ids = jnp.concatenate([corners[:, 0], corners[:, 1], order, lives]).astype(jnp.int32)

    turned = exchange(voltages, ALL)
    turned = turned.reshape(4, FREQS // 4, SLOTS, MINE, 2, signals, depth)
    *held, moments = correlate(ids, turned, depth * SLOTS)
    pieces = held[:1] + [swap(held[number], TM, SLOTS, number) for number in range(1, SLOTS)]

    rows = BLOCK // FREQS
    part = moments.reshape(SLOTS, 2, FREQS, rows, BLOCK).transpose(2, 0, 1, 3, 4)
    part = exchange(part.reshape(FREQS * SLOTS, 2 * rows, BLOCK), ALL)
    last, part = spread_sums(channel_mask, part, pieces[2], held[4])
    parts = exchange(part, FREQ)
    last = swap(last, TM, SLOTS, 3)
    planes = parts[:, : 2 * rows].reshape(FREQS, 2, rows, BLOCK).transpose(1, 0, 2, 3)
    ready = (parts[:, 2 * rows], planes.reshape(2, BLOCK, BLOCK), running_mean, running_var)
    outs = finish(PARTS[:4], 1 << 33, ids, channel_mask, ready, pieces, [])
    return tuple(finish(PARTS[4:], 1 << 20, ids, channel_mask, ready, [last], outs))


def solution(mesh):
    torus = Mesh(mesh.devices.reshape(SHAPE), ALL)
    return jax.shard_map(
        local,
        mesh=torus,
        in_specs=(
            P(None, None, FREQ, TM),
            P(),
            P(),
            P(FREQ),
            P(TM, None, None),
            P(TM, None, None),
        ),
        out_specs=(P(TM, FREQ, None, None, None, None), P(TM, FREQ, None, None)),
        check_vma=False,
    )
```

```python
import math

import jax
import jax.numpy as jnp
from jax import lax
from jax.experimental import pallas as pl
from jax.experimental.pallas import tpu as pltpu
from jax.sharding import Mesh, PartitionSpec as P

BLOCK = 128
mixing = 0.25

FREQ = ("y", "xh", "z")
TM = ("xl", "core")
ALL = FREQ + TM
SHAPE = (4, 2, 8, 2, 2)
SLOTS = 4
FREQS = 64
MINE = 2
BAND = BLOCK // 4
PLANES = (4, 2, BLOCK, BLOCK)
PARTS = ((0, 0, 2), (1, 0, 2), (2, 0, 2), (3, 0, 1), (3, 1, 1))


def nt(left, right):
    return lax.dot_general(
        left, right, (((1,), (1,)), ((), ())), preferred_element_type=jnp.float32
    )


def correlate_kernel(scale, ids, turned_ref, *refs):
    outs, moment_ref = refs[: len(PARTS)], refs[len(PARTS)]
    loaded, stage, load_sems, sems = refs[len(PARTS) + 1 :]
    blocks, per_block, pieces, _, _, signals, depth = turned_ref.shape
    width = per_block * signals

    def load(channel, block):
        return pltpu.make_async_copy(
            turned_ref.at[block, :, :, channel], loaded.at[channel, block], load_sems.at[channel, block]
        )

    def copy(number, channel):
        for out, (step, first, many) in zip(outs, PARTS):
            if step == number and first <= channel < first + many:
                return pltpu.make_async_copy(
                    stage.at[number, channel], out.at[channel - first], sems.at[number, channel]
                )

    def side(channel, block, part):
        return [
            loaded[channel, block, :, piece, part].reshape(width, depth) for piece in range(pieces)
        ]

    for channel in range(MINE):
        for block in range(blocks):
            load(channel, block).start()
    low, high = slice(0, BLOCK), slice(BLOCK, 2 * BLOCK)
    for channel in range(MINE):
        live = ids[3 * SLOTS + channel].astype(jnp.float32)
        for block in range(blocks):
            load(channel, block).wait()
        for number in range(SLOTS):
            row, col, slot = ids[number], ids[SLOTS + number], ids[2 * SLOTS + number]
            row_re, row_im = side(channel, row, 0), side(channel, row, 1)
            columns = jnp.concatenate(side(channel, col, 0) + side(channel, col, 1), axis=1)
            real = nt(jnp.concatenate(row_re + row_im, axis=1), columns) * scale
            minus_re = [-part for part in row_re]
            imag = nt(jnp.concatenate(row_im + minus_re, axis=1), columns) * scale
            i_re = real[low, low] + real[high, high]
            i_im = imag[low, low] + imag[high, high]
            stage[number, channel, 0, 0] = i_re
            stage[number, channel, 0, 1] = i_im
            stage[number, channel, 1, 0] = real[low, low] - real[high, high]
            stage[number, channel, 1, 1] = imag[low, low] - imag[high, high]
            stage[number, channel, 2, 0] = real[low, high] + real[high, low]
            stage[number, channel, 2, 1] = imag[low, high] + imag[high, low]
            stage[number, channel, 3, 0] = imag[low, high] - imag[high, low]
            stage[number, channel, 3, 1] = real[high, low] - real[low, high]
            copy(number, channel).start()
            power = i_re * i_re + i_im * i_im
            masked = power * live
            for order, plane in enumerate((masked, masked * power)):
                if channel > 0:
                    plane = plane + moment_ref[slot, order]
                moment_ref[slot, order] = plane
    for channel in range(MINE):
        for number in range(SLOTS):
            copy(number, channel).wait()


def correlate(ids, turned, samples):
    blocks, per_block, pieces, channels, _, signals, depth = turned.shape
    anywhere = pl.BlockSpec(memory_space=pl.ANY)
    return pl.pallas_call(
        lambda *refs: correlate_kernel(1.0 / math.sqrt(samples), *refs),
        in_specs=[pl.BlockSpec(memory_space=pltpu.SMEM), anywhere],
        out_specs=[anywhere] * len(PARTS) + [pl.BlockSpec(memory_space=pltpu.VMEM)],
        scratch_shapes=[
            pltpu.VMEM((channels, blocks, per_block, pieces, 2, signals, depth), turned.dtype),
            pltpu.VMEM((SLOTS, channels) + PLANES, jnp.float32),
            pltpu.SemaphoreType.DMA((channels, blocks)),
            pltpu.SemaphoreType.DMA((SLOTS, channels)),
        ],
        out_shape=[jax.ShapeDtypeStruct((many,) + PLANES, jnp.float32) for _, _, many in PARTS]
        + [jax.ShapeDtypeStruct((SLOTS, 2, BLOCK, BLOCK), jnp.float32)],
        compiler_params=pltpu.CompilerParams(vmem_limit_bytes=56 << 20),
        cost_estimate=pl.CostEstimate(
            flops=SLOTS * channels * 8 * (2 * BLOCK) ** 2 * samples,
            bytes_accessed=13 << 20,
            transcendentals=0,
        ),
        name="correlate",
    )(ids, turned)


def spread_kernel(mask, bands_ref, _, held_ref, passed_ref, part_ref, sem):
    passed = pltpu.make_async_copy(held_ref, passed_ref, sem)
    passed.start()
    total = jnp.sum(bands_ref[...], axis=0)
    live = mask[0]
    for index in range(1, mask.shape[0]):
        live = live + mask[index]
    rows = total.shape[0]
    row = jnp.full((1, BLOCK), live.astype(jnp.float32))
    for receiver in range(part_ref.shape[0]):
        part_ref[receiver, :rows] = total
        part_ref[receiver, rows:] = row
    passed.wait()


def spread_sums(mask, bands, earlier, held):
    whole = pl.BlockSpec(memory_space=pltpu.VMEM)
    anywhere = pl.BlockSpec(memory_space=pl.ANY)
    return pl.pallas_call(
        spread_kernel,
        in_specs=[
            pl.BlockSpec(memory_space=pltpu.SMEM),
            whole,
            pl.BlockSpec(memory_space=pltpu.HBM),
            anywhere,
        ],
        out_specs=[whole] * 2,
        out_shape=[
            jax.ShapeDtypeStruct(held.shape, jnp.float32),
            jax.ShapeDtypeStruct((FREQS, bands.shape[1] + 1, BLOCK), jnp.float32),
        ],
        scratch_shapes=[pltpu.SemaphoreType.DMA],
        cost_estimate=pl.CostEstimate(flops=1 << 18, bytes_accessed=1 << 20, transcendentals=0),
        name="spread_sums",
    )(mask, bands, earlier, held)


def moving_kernel(parts, ids, *refs):
    pieces, (stokes_ref, power_ref, loaded, sems) = refs[: len(parts)], refs[len(parts) :]
    loads, copies = [], []
    for index, (_, _, many) in enumerate(parts):
        loads.append(
            pltpu.make_async_copy(pieces[index], loaded.at[index, pl.ds(0, many)], sems.at[index, 0])
        )
        loads[-1].start()
    for index, (step, start, many) in enumerate(parts):
        span = pl.ds(MINE * ids[2 * SLOTS + step] + start, many)
        loads[index].wait()
        copies.append(
            pltpu.make_async_copy(
                loaded.at[index, pl.ds(0, many)], stokes_ref.at[0, span], sems.at[index, 1]
            )
        )
        copies[-1].start()
        for channel in range(many):
            i_re, i_im = loaded[index, channel, 0, 0], loaded[index, channel, 0, 1]
            power_ref[index, channel] = i_re * i_re + i_im * i_im
    for copy in copies:
        copy.wait()


def place(parts, ids, pieces):
    placed = pl.BlockSpec(memory_space=pltpu.HBM)
    count = len(parts)
    return pl.pallas_call(
        lambda *refs: moving_kernel(parts, *refs),
        in_specs=[pl.BlockSpec(memory_space=pltpu.SMEM)] + [placed] * count,
        out_specs=[placed, pl.BlockSpec(memory_space=pltpu.VMEM)],
        out_shape=[
            jax.ShapeDtypeStruct((1, MINE * SLOTS) + PLANES, jnp.float32),
            jax.ShapeDtypeStruct((count, MINE, BLOCK, BLOCK), jnp.float32),
        ],
        scratch_shapes=[
            pltpu.VMEM((count, MINE) + PLANES, jnp.float32),
            pltpu.SemaphoreType.DMA((count, 2)),
        ],
        compiler_params=pltpu.CompilerParams(vmem_limit_bytes=16 << 20),
        cost_estimate=pl.CostEstimate(
            flops=count << 17, bytes_accessed=count << 21, transcendentals=0
        ),
        name="place",
    )(ids, *pieces)


def bands_of(count_ref, planes_ref, mean_ref, var_ref):
    count = jnp.sum(count_ref[...], axis=0, keepdims=True)
    bands = []
    for band in range(BLOCK // BAND):
        rows = slice(band * BAND, (band + 1) * BAND)
        first = planes_ref[0, rows] / count
        second = planes_ref[1, rows] / count
        mean = mean_ref[0, rows]
        blended = (1.0 - mixing) * mean + mixing * first
        spread = (
            (1.0 - mixing) * var_ref[0, rows]
            + mixing * (second - first * first)
            + mixing * (1.0 - mixing) * (first - mean) ** 2
        )
        bands.append((rows, blended, spread))
    return bands


def weigh_kernel(parts, ids, mask, count_ref, planes_ref, mean_ref, var_ref, *refs):
    power_ref, weight_ref, stage, sems = refs
    copies = []
    bands = bands_of(count_ref, planes_ref, mean_ref, var_ref)
    for index, (step, start, many) in enumerate(parts):
        place = MINE * ids[2 * SLOTS + step] + start
        for channel in range(many):
            live = mask[place + channel].astype(jnp.float32)
            for rows, blended, spread in bands:
                off = power_ref[index, channel, rows] - blended
                stage[index, channel, rows] = live / (1.0 + off * off / spread)
        copies.append(
            pltpu.make_async_copy(
                stage.at[index, pl.ds(0, many)],
                weight_ref.at[0, pl.ds(place, many)],
                sems.at[index],
            )
        )
        copies[-1].start()
    for copy in copies:
        copy.wait()


def weigh(parts, cost, ids, mask, ready, powers):
    whole = pl.BlockSpec(memory_space=pltpu.VMEM)
    scalars = pl.BlockSpec(memory_space=pltpu.SMEM)
    count = len(parts)
    return pl.pallas_call(
        lambda *refs: weigh_kernel(parts, *refs),
        in_specs=[scalars] * 2 + [whole] * 5,
        out_specs=pl.BlockSpec(memory_space=pltpu.HBM),
        out_shape=jax.ShapeDtypeStruct((1, MINE * SLOTS, BLOCK, BLOCK), jnp.float32),
        scratch_shapes=[
            pltpu.VMEM((count, MINE, BLOCK, BLOCK), jnp.float32),
            pltpu.SemaphoreType.DMA((count,)),
        ],
        compiler_params=pltpu.CompilerParams(vmem_limit_bytes=16 << 20),
        cost_estimate=pl.CostEstimate(flops=cost, bytes_accessed=1 << 20, transcendentals=0),
        name="weigh",
    )(ids, mask, *ready, powers)


def finish_kernel(parts, ids, mask, count_ref, planes_ref, mean_ref, var_ref, *refs):
    pieces, (stokes_ref, weight_ref, loaded, stage, sems) = refs[: len(parts)], refs[-5:]
    loads, copies = [], []
    for index, (_, _, many) in enumerate(parts):
        loads.append(
            pltpu.make_async_copy(pieces[index], loaded.at[index, pl.ds(0, many)], sems.at[index, 0])
        )
        loads[-1].start()
    bands = bands_of(count_ref, planes_ref, mean_ref, var_ref)
    for index, (step, start, many) in enumerate(parts):
        place = MINE * ids[2 * SLOTS + step] + start
        span, held = pl.ds(place, many), pl.ds(0, many)
        loads[index].wait()
        copies.append(
            pltpu.make_async_copy(
                loaded.at[index, held], stokes_ref.at[0, span], sems.at[index, 1]
            )
        )
        copies[-1].start()
        for channel in range(many):
            live = mask[place + channel].astype(jnp.float32)
            for rows, blended, spread in bands:
                i_re, i_im = loaded[index, channel, 0, 0, rows], loaded[index, channel, 0, 1, rows]
                off = i_re * i_re + i_im * i_im - blended
                stage[index, channel, rows] = live / (1.0 + off * off / spread)
        copies.append(
            pltpu.make_async_copy(stage.at[index, held], weight_ref.at[0, span], sems.at[index, 2])
        )
        copies[-1].start()
    for copy in copies:
        copy.wait()


def finish(parts, cost, ids, mask, ready, pieces, outs):
    whole = pl.BlockSpec(memory_space=pltpu.VMEM)
    scalars = pl.BlockSpec(memory_space=pltpu.SMEM)
    placed = pl.BlockSpec(memory_space=pltpu.HBM)
    count = len(parts)
    return pl.pallas_call(
        lambda *refs: finish_kernel(parts, *refs),
        in_specs=[scalars] * 2
        + [whole] * 4
        + [placed] * count
        + [placed] * len(outs),
        out_specs=[placed] * 2,
        out_shape=[
            jax.ShapeDtypeStruct((1, MINE * SLOTS) + PLANES, jnp.float32),
            jax.ShapeDtypeStruct((1, MINE * SLOTS, BLOCK, BLOCK), jnp.float32),
        ],
        input_output_aliases={6 + count + index: index for index in range(len(outs))},
        scratch_shapes=[
            pltpu.VMEM((count, MINE) + PLANES, jnp.float32),
            pltpu.VMEM((count, MINE, BLOCK, BLOCK), jnp.float32),
            pltpu.SemaphoreType.DMA((count, 3)),
        ],
        compiler_params=pltpu.CompilerParams(vmem_limit_bytes=16 << 20),
        cost_estimate=pl.CostEstimate(
            flops=cost, bytes_accessed=count << 21, transcendentals=0
        ),
        name=f"finish_{count}",
    )(ids, mask, *ready, *pieces, *outs)


def swap(value, names, size, step):
    return lax.ppermute(value, names, [(i, i ^ step) for i in range(size)])


def exchange(value, names):
    return lax.all_to_all(value, names, split_axis=0, concat_axis=0, tiled=True)


def local(voltages, pattern, owner_map, channel_mask, running_mean, running_var):
    total, _, signals, depth = voltages.shape
    own = lax.axis_index(TM)
    slots = jnp.arange(SLOTS, dtype=jnp.int32)
    order = own ^ slots
    tiles = jnp.sum(jnp.where(order[:, None] == slots[None], owner_map[None], 0), axis=1)
    corners = jnp.sum(jnp.where((tiles[:, None] == slots[None])[..., None], pattern[None], 0), axis=1)
    lives = jnp.sum(
        jnp.where(own == slots[:, None], channel_mask.reshape(SLOTS, MINE), 0), axis=0
    )
    ids = jnp.concatenate([corners[:, 0], corners[:, 1], order, lives]).astype(jnp.int32)

    turned = exchange(voltages, ALL)
    turned = turned.reshape(4, FREQS // 4, SLOTS, MINE, 2, signals, depth)
    *held, moments = correlate(ids, turned, depth * SLOTS)
    pieces = held[:1] + [swap(held[number], TM, SLOTS, number) for number in range(1, SLOTS)]

    rows = BLOCK // FREQS
    part = moments.reshape(SLOTS, 2, FREQS, rows, BLOCK).transpose(2, 0, 1, 3, 4)
    part = exchange(part.reshape(FREQS * SLOTS, 2 * rows, BLOCK), ALL)
    last, part = spread_sums(channel_mask, part, pieces[2], held[4])
    parts = exchange(part, FREQ)
    last = swap(last, TM, SLOTS, 3)
    planes = parts[:, : 2 * rows].reshape(FREQS, 2, rows, BLOCK).transpose(1, 0, 2, 3)
    ready = (parts[:, 2 * rows], planes.reshape(2, BLOCK, BLOCK), running_mean, running_var)
    stokes, powers = place(PARTS[:4], ids, pieces)
    weights = weigh(PARTS[:4], 1 << 33, ids, channel_mask, ready, powers)
    return tuple(
        finish(PARTS[4:], 1 << 20, ids, channel_mask, ready, [last], [stokes, weights])
    )


def solution(mesh):
    torus = Mesh(mesh.devices.reshape(SHAPE), ALL)
    return jax.shard_map(
        local,
        mesh=torus,
        in_specs=(
            P(None, None, FREQ, TM),
            P(),
            P(),
            P(FREQ),
            P(TM, None, None),
            P(TM, None, None),
        ),
        out_specs=(P(TM, FREQ, None, None, None, None), P(TM, FREQ, None, None)),
        check_vma=False,
    )
```

```python
import math

import jax
import jax.numpy as jnp
from jax import lax
from jax.experimental import pallas as pl
from jax.experimental.pallas import tpu as pltpu
from jax.sharding import Mesh, PartitionSpec as P

BLOCK = 128
mixing = 0.25

FREQ = ("y", "xh", "z")
TM = ("xl", "core")
ALL = FREQ + TM
SHAPE = (4, 2, 8, 2, 2)
SLOTS = 4
FREQS = 64
MINE = 2
BAND = BLOCK // 4
PLANES = (4, 2, BLOCK, BLOCK)
PARTS = ((0, 0, 2), (1, 0, 2), (2, 0, 2), (3, 0, 1), (3, 1, 1))


def nt(left, right):
    return lax.dot_general(
        left, right, (((1,), (1,)), ((), ())), preferred_element_type=jnp.float32
    )


def correlate_kernel(scale, steps, ids, turned_ref, *refs):
    refs = list(refs)
    early_ref = refs.pop(0) if len(steps) > 1 else None
    kept = [part for part in PARTS if part[0] in steps]
    outs, moment_ref = refs[: len(kept)], refs[len(kept)]
    loaded, stage, load_sems, sems = refs[len(kept) + 1 :]
    _, per_block, pieces, _, _, signals, depth = turned_ref.shape
    width = per_block * signals
    places = loaded.shape[1]
    low, high = slice(0, BLOCK), slice(BLOCK, 2 * BLOCK)

    def load(channel, place):
        block = place if early_ref is not None else ids[steps[0] + place * SLOTS]
        return pltpu.make_async_copy(
            turned_ref.at[block, :, :, channel], loaded.at[channel, place], load_sems.at[channel, place]
        )

    def copy(index, channel):
        for out, (step, first, many) in zip(outs, kept):
            if step == steps[index] and first <= channel < first + many:
                return pltpu.make_async_copy(
                    stage.at[index, channel], out.at[channel - first], sems.at[index, channel]
                )

    def side(channel, place, part):
        return [
            loaded[channel, place, :, piece, part].reshape(width, depth) for piece in range(pieces)
        ]

    for channel in range(MINE):
        for place in range(places):
            load(channel, place).start()
    if early_ref is not None:
        for step in set(range(SLOTS)) - set(steps):
            moment_ref[ids[2 * SLOTS + step]] = early_ref[0]
    for channel in range(MINE):
        live = ids[3 * SLOTS + channel].astype(jnp.float32)
        for place in range(places):
            load(channel, place).wait()
        for index, step in enumerate(steps):
            row, col, slot = (
                (0, 1, 0)
                if early_ref is None
                else (ids[step], ids[SLOTS + step], ids[2 * SLOTS + step])
            )
            row_re, row_im = side(channel, row, 0), side(channel, row, 1)
            columns = jnp.concatenate(side(channel, col, 0) + side(channel, col, 1), axis=1)
            real = nt(jnp.concatenate(row_re + row_im, axis=1), columns) * scale
            minus_re = [-part for part in row_re]
            imag = nt(jnp.concatenate(row_im + minus_re, axis=1), columns) * scale
            i_re = real[low, low] + real[high, high]
            i_im = imag[low, low] + imag[high, high]
            stage[index, channel, 0, 0] = i_re
            stage[index, channel, 0, 1] = i_im
            stage[index, channel, 1, 0] = real[low, low] - real[high, high]
            stage[index, channel, 1, 1] = imag[low, low] - imag[high, high]
            stage[index, channel, 2, 0] = real[low, high] + real[high, low]
            stage[index, channel, 2, 1] = imag[low, high] + imag[high, low]
            stage[index, channel, 3, 0] = imag[low, high] - imag[high, low]
            stage[index, channel, 3, 1] = real[high, low] - real[low, high]
            copy(index, channel).start()
            power = i_re * i_re + i_im * i_im
            masked = power * live
            for order, plane in enumerate((masked, masked * power)):
                if channel > 0:
                    plane = plane + moment_ref[slot, order]
                moment_ref[slot, order] = plane
    for channel in range(MINE):
        for index in range(len(steps)):
            copy(index, channel).wait()


def correlate(steps, ids, turned, early, samples):
    blocks, per_block, pieces, channels, _, signals, depth = turned.shape
    kept = [part for part in PARTS if part[0] in steps]
    many = len(steps)
    places, slots = (blocks, SLOTS) if many > 1 else (2, 1)
    anywhere = pl.BlockSpec(memory_space=pl.ANY)
    whole = pl.BlockSpec(memory_space=pltpu.VMEM)
    return pl.pallas_call(
        lambda *refs: correlate_kernel(1.0 / math.sqrt(samples), steps, *refs),
        in_specs=[pl.BlockSpec(memory_space=pltpu.SMEM), anywhere] + [whole] * len(early),
        out_specs=[anywhere] * len(kept) + [whole],
        scratch_shapes=[
            pltpu.VMEM((channels, places, per_block, pieces, 2, signals, depth), turned.dtype),
            pltpu.VMEM((many, channels) + PLANES, jnp.float32),
            pltpu.SemaphoreType.DMA((channels, places)),
            pltpu.SemaphoreType.DMA((many, channels)),
        ],
        out_shape=[jax.ShapeDtypeStruct((count,) + PLANES, jnp.float32) for _, _, count in kept]
        + [jax.ShapeDtypeStruct((slots, 2, BLOCK, BLOCK), jnp.float32)],
        compiler_params=pltpu.CompilerParams(vmem_limit_bytes=56 << 20),
        cost_estimate=pl.CostEstimate(
            flops=many * channels * 8 * (2 * BLOCK) ** 2 * samples,
            bytes_accessed=(places + many) * channels << 20,
            transcendentals=0,
        ),
        name=f"correlate_{many}",
    )(ids, turned, *early)


def spread_kernel(mask, bands_ref, _, held_ref, passed_ref, part_ref, sem):
    passed = pltpu.make_async_copy(held_ref, passed_ref, sem)
    passed.start()
    total = jnp.sum(bands_ref[...], axis=0)
    live = mask[0]
    for index in range(1, mask.shape[0]):
        live = live + mask[index]
    rows = total.shape[0]
    row = jnp.full((1, BLOCK), live.astype(jnp.float32))
    for receiver in range(part_ref.shape[0]):
        part_ref[receiver, :rows] = total
        part_ref[receiver, rows:] = row
    passed.wait()


def spread_sums(mask, bands, earlier, held):
    whole = pl.BlockSpec(memory_space=pltpu.VMEM)
    anywhere = pl.BlockSpec(memory_space=pl.ANY)
    return pl.pallas_call(
        spread_kernel,
        in_specs=[
            pl.BlockSpec(memory_space=pltpu.SMEM),
            whole,
            pl.BlockSpec(memory_space=pltpu.HBM),
            anywhere,
        ],
        out_specs=[whole] * 2,
        out_shape=[
            jax.ShapeDtypeStruct(held.shape, jnp.float32),
            jax.ShapeDtypeStruct((FREQS, bands.shape[1] + 1, BLOCK), jnp.float32),
        ],
        scratch_shapes=[pltpu.SemaphoreType.DMA],
        cost_estimate=pl.CostEstimate(flops=1 << 18, bytes_accessed=1 << 20, transcendentals=0),
        name="spread_sums",
    )(mask, bands, earlier, held)


def moving_kernel(parts, ids, *refs):
    pieces, (stokes_ref, power_ref, loaded, sems) = refs[: len(parts)], refs[len(parts) :]
    loads, copies = [], []
    for index, (_, _, many) in enumerate(parts):
        loads.append(
            pltpu.make_async_copy(pieces[index], loaded.at[index, pl.ds(0, many)], sems.at[index, 0])
        )
        loads[-1].start()
    for index, (step, start, many) in enumerate(parts):
        span = pl.ds(MINE * ids[2 * SLOTS + step] + start, many)
        loads[index].wait()
        copies.append(
            pltpu.make_async_copy(
                loaded.at[index, pl.ds(0, many)], stokes_ref.at[0, span], sems.at[index, 1]
            )
        )
        copies[-1].start()
        for channel in range(many):
            i_re, i_im = loaded[index, channel, 0, 0], loaded[index, channel, 0, 1]
            power_ref[index, channel] = i_re * i_re + i_im * i_im
    for copy in copies:
        copy.wait()


def place(parts, ids, pieces):
    placed = pl.BlockSpec(memory_space=pltpu.HBM)
    count = len(parts)
    return pl.pallas_call(
        lambda *refs: moving_kernel(parts, *refs),
        in_specs=[pl.BlockSpec(memory_space=pltpu.SMEM)] + [placed] * count,
        out_specs=[placed, pl.BlockSpec(memory_space=pltpu.VMEM)],
        out_shape=[
            jax.ShapeDtypeStruct((1, MINE * SLOTS) + PLANES, jnp.float32),
            jax.ShapeDtypeStruct((count, MINE, BLOCK, BLOCK), jnp.float32),
        ],
        scratch_shapes=[
            pltpu.VMEM((count, MINE) + PLANES, jnp.float32),
            pltpu.SemaphoreType.DMA((count, 2)),
        ],
        compiler_params=pltpu.CompilerParams(vmem_limit_bytes=16 << 20),
        cost_estimate=pl.CostEstimate(
            flops=count << 17, bytes_accessed=count << 21, transcendentals=0
        ),
        name="place",
    )(ids, *pieces)


def bands_of(count_ref, planes_ref, mean_ref, var_ref):
    count = jnp.sum(count_ref[...], axis=0, keepdims=True)
    bands = []
    for band in range(BLOCK // BAND):
        rows = slice(band * BAND, (band + 1) * BAND)
        first = planes_ref[0, rows] / count
        second = planes_ref[1, rows] / count
        mean = mean_ref[0, rows]
        blended = (1.0 - mixing) * mean + mixing * first
        spread = (
            (1.0 - mixing) * var_ref[0, rows]
            + mixing * (second - first * first)
            + mixing * (1.0 - mixing) * (first - mean) ** 2
        )
        bands.append((rows, blended, spread))
    return bands


def weigh_kernel(parts, ids, mask, count_ref, planes_ref, mean_ref, var_ref, *refs):
    power_ref, weight_ref, stage, sems = refs
    copies = []
    bands = bands_of(count_ref, planes_ref, mean_ref, var_ref)
    for index, (step, start, many) in enumerate(parts):
        place = MINE * ids[2 * SLOTS + step] + start
        for channel in range(many):
            live = mask[place + channel].astype(jnp.float32)
            for rows, blended, spread in bands:
                off = power_ref[index, channel, rows] - blended
                stage[index, channel, rows] = live / (1.0 + off * off / spread)
        copies.append(
            pltpu.make_async_copy(
                stage.at[index, pl.ds(0, many)],
                weight_ref.at[0, pl.ds(place, many)],
                sems.at[index],
            )
        )
        copies[-1].start()
    for copy in copies:
        copy.wait()


def weigh(parts, cost, ids, mask, ready, powers):
    whole = pl.BlockSpec(memory_space=pltpu.VMEM)
    scalars = pl.BlockSpec(memory_space=pltpu.SMEM)
    count = len(parts)
    return pl.pallas_call(
        lambda *refs: weigh_kernel(parts, *refs),
        in_specs=[scalars] * 2 + [whole] * 5,
        out_specs=pl.BlockSpec(memory_space=pltpu.HBM),
        out_shape=jax.ShapeDtypeStruct((1, MINE * SLOTS, BLOCK, BLOCK), jnp.float32),
        scratch_shapes=[
            pltpu.VMEM((count, MINE, BLOCK, BLOCK), jnp.float32),
            pltpu.SemaphoreType.DMA((count,)),
        ],
        compiler_params=pltpu.CompilerParams(vmem_limit_bytes=16 << 20),
        cost_estimate=pl.CostEstimate(flops=cost, bytes_accessed=1 << 20, transcendentals=0),
        name="weigh",
    )(ids, mask, *ready, powers)


def finish_kernel(parts, ids, mask, count_ref, planes_ref, mean_ref, var_ref, *refs):
    pieces, (stokes_ref, weight_ref, loaded, stage, sems) = refs[: len(parts)], refs[-5:]
    loads, copies = [], []
    for index, (_, _, many) in enumerate(parts):
        loads.append(
            pltpu.make_async_copy(pieces[index], loaded.at[index, pl.ds(0, many)], sems.at[index, 0])
        )
        loads[-1].start()
    bands = bands_of(count_ref, planes_ref, mean_ref, var_ref)
    for index, (step, start, many) in enumerate(parts):
        place = MINE * ids[2 * SLOTS + step] + start
        span, held = pl.ds(place, many), pl.ds(0, many)
        loads[index].wait()
        copies.append(
            pltpu.make_async_copy(
                loaded.at[index, held], stokes_ref.at[0, span], sems.at[index, 1]
            )
        )
        copies[-1].start()
        for channel in range(many):
            live = mask[place + channel].astype(jnp.float32)
            for rows, blended, spread in bands:
                i_re, i_im = loaded[index, channel, 0, 0, rows], loaded[index, channel, 0, 1, rows]
                off = i_re * i_re + i_im * i_im - blended
                stage[index, channel, rows] = live / (1.0 + off * off / spread)
        copies.append(
            pltpu.make_async_copy(stage.at[index, held], weight_ref.at[0, span], sems.at[index, 2])
        )
        copies[-1].start()
    for copy in copies:
        copy.wait()


def finish(parts, cost, ids, mask, ready, pieces, outs):
    whole = pl.BlockSpec(memory_space=pltpu.VMEM)
    scalars = pl.BlockSpec(memory_space=pltpu.SMEM)
    placed = pl.BlockSpec(memory_space=pltpu.HBM)
    count = len(parts)
    return pl.pallas_call(
        lambda *refs: finish_kernel(parts, *refs),
        in_specs=[scalars] * 2
        + [whole] * 4
        + [placed] * count
        + [placed] * len(outs),
        out_specs=[placed] * 2,
        out_shape=[
            jax.ShapeDtypeStruct((1, MINE * SLOTS) + PLANES, jnp.float32),
            jax.ShapeDtypeStruct((1, MINE * SLOTS, BLOCK, BLOCK), jnp.float32),
        ],
        input_output_aliases={6 + count + index: index for index in range(len(outs))},
        scratch_shapes=[
            pltpu.VMEM((count, MINE) + PLANES, jnp.float32),
            pltpu.VMEM((count, MINE, BLOCK, BLOCK), jnp.float32),
            pltpu.SemaphoreType.DMA((count, 3)),
        ],
        compiler_params=pltpu.CompilerParams(vmem_limit_bytes=16 << 20),
        cost_estimate=pl.CostEstimate(
            flops=cost, bytes_accessed=count << 21, transcendentals=0
        ),
        name=f"finish_{count}",
    )(ids, mask, *ready, *pieces, *outs)


def swap(value, names, size, step):
    return lax.ppermute(value, names, [(i, i ^ step) for i in range(size)])


def exchange(value, names):
    return lax.all_to_all(value, names, split_axis=0, concat_axis=0, tiled=True)


def local(voltages, pattern, owner_map, channel_mask, running_mean, running_var):
    total, _, signals, depth = voltages.shape
    own = lax.axis_index(TM)
    slots = jnp.arange(SLOTS, dtype=jnp.int32)
    order = own ^ slots
    tiles = jnp.sum(jnp.where(order[:, None] == slots[None], owner_map[None], 0), axis=1)
    corners = jnp.sum(jnp.where((tiles[:, None] == slots[None])[..., None], pattern[None], 0), axis=1)
    lives = jnp.sum(
        jnp.where(own == slots[:, None], channel_mask.reshape(SLOTS, MINE), 0), axis=0
    )
    ids = jnp.concatenate([corners[:, 0], corners[:, 1], order, lives]).astype(jnp.int32)

    turned = exchange(voltages, ALL)
    turned = turned.reshape(4, FREQS // 4, SLOTS, MINE, 2, signals, depth)
    crossing, early = correlate((2,), ids, turned, [], depth * SLOTS)
    *held, moments = correlate((0, 1, 3), ids, turned, [early], depth * SLOTS)
    held.insert(2, crossing)
    pieces = held[:1] + [swap(held[number], TM, SLOTS, number) for number in range(1, SLOTS)]

    rows = BLOCK // FREQS
    part = moments.reshape(SLOTS, 2, FREQS, rows, BLOCK).transpose(2, 0, 1, 3, 4)
    part = exchange(part.reshape(FREQS * SLOTS, 2 * rows, BLOCK), ALL)
    last, part = spread_sums(channel_mask, part, pieces[2], held[4])
    parts = exchange(part, FREQ)
    last = swap(last, TM, SLOTS, 3)
    planes = parts[:, : 2 * rows].reshape(FREQS, 2, rows, BLOCK).transpose(1, 0, 2, 3)
    ready = (parts[:, 2 * rows], planes.reshape(2, BLOCK, BLOCK), running_mean, running_var)
    stokes, powers = place(PARTS[:4], ids, pieces)
    weights = weigh(PARTS[:4], 1 << 33, ids, channel_mask, ready, powers)
    return tuple(
        finish(PARTS[4:], 1 << 20, ids, channel_mask, ready, [last], [stokes, weights])
    )


def solution(mesh):
    torus = Mesh(mesh.devices.reshape(SHAPE), ALL)
    return jax.shard_map(
        local,
        mesh=torus,
        in_specs=(
            P(None, None, FREQ, TM),
            P(),
            P(),
            P(FREQ),
            P(TM, None, None),
            P(TM, None, None),
        ),
        out_specs=(P(TM, FREQ, None, None, None, None), P(TM, FREQ, None, None)),
        check_vma=False,
    )
```

```python
import math

import jax
import jax.numpy as jnp
from jax import lax
from jax.experimental import pallas as pl
from jax.experimental.pallas import tpu as pltpu
from jax.sharding import Mesh, PartitionSpec as P

BLOCK = 128
mixing = 0.25

FREQ = ("y", "xh", "z")
TM = ("xl", "core")
ALL = FREQ + TM
SHAPE = (4, 2, 8, 2, 2)
SLOTS = 4
FREQS = 64
MINE = 2
BAND = BLOCK // 4
PLANES = (4, 2, BLOCK, BLOCK)
PARTS = ((0, 0, 2), (1, 0, 2), (2, 0, 2), (3, 0, 1), (3, 1, 1))


def nt(left, right):
    return lax.dot_general(
        left, right, (((1,), (1,)), ((), ())), preferred_element_type=jnp.float32
    )


def correlate_kernel(scale, steps, ids, turned_ref, *refs):
    refs = list(refs)
    early_ref = refs.pop(0) if len(steps) > 1 else None
    kept = [part for part in PARTS if part[0] in steps]
    outs, sum_ref = refs[: len(kept)], refs[len(kept)]
    loaded, stage, load_sems, sems = refs[len(kept) + 1 : len(kept) + 5]
    moment_ref = sum_ref if early_ref is None else refs[-1]
    _, per_block, pieces, _, _, signals, depth = turned_ref.shape
    width = per_block * signals
    places = loaded.shape[1]
    low, high = slice(0, BLOCK), slice(BLOCK, 2 * BLOCK)

    def load(channel, place):
        block = place if early_ref is not None else ids[steps[0] + place * SLOTS]
        return pltpu.make_async_copy(
            turned_ref.at[block, :, :, channel], loaded.at[channel, place], load_sems.at[channel, place]
        )

    def copy(index, channel):
        for out, (step, first, many) in zip(outs, kept):
            if step == steps[index] and first <= channel < first + many:
                return pltpu.make_async_copy(
                    stage.at[index, channel], out.at[channel - first], sems.at[index, channel]
                )

    def side(channel, place, part):
        return [
            loaded[channel, place, :, piece, part].reshape(width, depth) for piece in range(pieces)
        ]

    for channel in range(MINE):
        for place in range(places):
            load(channel, place).start()
    if early_ref is not None:
        for step in set(range(SLOTS)) - set(steps):
            moment_ref[ids[2 * SLOTS + step]] = early_ref[0]
    for channel in range(MINE):
        live = ids[3 * SLOTS + channel].astype(jnp.float32)
        for place in range(places):
            load(channel, place).wait()
        for index, step in enumerate(steps):
            row, col, slot = (
                (0, 1, 0)
                if early_ref is None
                else (ids[step], ids[SLOTS + step], ids[2 * SLOTS + step])
            )
            row_re, row_im = side(channel, row, 0), side(channel, row, 1)
            columns = jnp.concatenate(side(channel, col, 0) + side(channel, col, 1), axis=1)
            real = nt(jnp.concatenate(row_re + row_im, axis=1), columns) * scale
            minus_re = [-part for part in row_re]
            imag = nt(jnp.concatenate(row_im + minus_re, axis=1), columns) * scale
            i_re = real[low, low] + real[high, high]
            i_im = imag[low, low] + imag[high, high]
            stage[index, channel, 0, 0] = i_re
            stage[index, channel, 0, 1] = i_im
            stage[index, channel, 1, 0] = real[low, low] - real[high, high]
            stage[index, channel, 1, 1] = imag[low, low] - imag[high, high]
            stage[index, channel, 2, 0] = real[low, high] + real[high, low]
            stage[index, channel, 2, 1] = imag[low, high] + imag[high, low]
            stage[index, channel, 3, 0] = imag[low, high] - imag[high, low]
            stage[index, channel, 3, 1] = real[high, low] - real[low, high]
            copy(index, channel).start()
            power = i_re * i_re + i_im * i_im
            masked = power * live
            for order, plane in enumerate((masked, masked * power)):
                if channel > 0:
                    plane = plane + moment_ref[slot, order]
                moment_ref[slot, order] = plane
    if early_ref is not None:
        rows = BLOCK // FREQS
        for slot in range(SLOTS):
            for order in range(2):
                sum_ref[:, slot, pl.ds(order * rows, rows)] = moment_ref[slot, order].reshape(
                    FREQS, rows, BLOCK
                )
    for channel in range(MINE):
        for index in range(len(steps)):
            copy(index, channel).wait()


def correlate(steps, ids, turned, early, samples):
    blocks, per_block, pieces, channels, _, signals, depth = turned.shape
    kept = [part for part in PARTS if part[0] in steps]
    many = len(steps)
    places = blocks if many > 1 else 2
    sums = (FREQS, SLOTS, 2 * BLOCK // FREQS, BLOCK) if many > 1 else (1, 2, BLOCK, BLOCK)
    anywhere = pl.BlockSpec(memory_space=pl.ANY)
    whole = pl.BlockSpec(memory_space=pltpu.VMEM)
    return pl.pallas_call(
        lambda *refs: correlate_kernel(1.0 / math.sqrt(samples), steps, *refs),
        in_specs=[pl.BlockSpec(memory_space=pltpu.SMEM), anywhere] + [whole] * len(early),
        out_specs=[anywhere] * len(kept) + [whole],
        scratch_shapes=[
            pltpu.VMEM((channels, places, per_block, pieces, 2, signals, depth), turned.dtype),
            pltpu.VMEM((many, channels) + PLANES, jnp.float32),
            pltpu.SemaphoreType.DMA((channels, places)),
            pltpu.SemaphoreType.DMA((many, channels)),
        ]
        + [pltpu.VMEM((SLOTS, 2, BLOCK, BLOCK), jnp.float32)] * len(early),
        out_shape=[jax.ShapeDtypeStruct((count,) + PLANES, jnp.float32) for _, _, count in kept]
        + [jax.ShapeDtypeStruct(sums, jnp.float32)],
        compiler_params=pltpu.CompilerParams(vmem_limit_bytes=56 << 20),
        cost_estimate=pl.CostEstimate(
            flops=many * channels * 8 * (2 * BLOCK) ** 2 * samples,
            bytes_accessed=(places + many) * channels << 20,
            transcendentals=0,
        ),
        name=f"correlate_{many}",
    )(ids, turned, *early)


def spread_kernel(mask, bands_ref, _, held_ref, passed_ref, part_ref, sem):
    passed = pltpu.make_async_copy(held_ref, passed_ref, sem)
    passed.start()
    total = jnp.sum(bands_ref[...], axis=0)
    live = mask[0]
    for index in range(1, mask.shape[0]):
        live = live + mask[index]
    rows = total.shape[0]
    row = jnp.full((1, BLOCK), live.astype(jnp.float32))
    for receiver in range(part_ref.shape[0]):
        part_ref[receiver, :rows] = total
        part_ref[receiver, rows:] = row
    passed.wait()


def spread_sums(mask, bands, earlier, held):
    whole = pl.BlockSpec(memory_space=pltpu.VMEM)
    anywhere = pl.BlockSpec(memory_space=pl.ANY)
    return pl.pallas_call(
        spread_kernel,
        in_specs=[
            pl.BlockSpec(memory_space=pltpu.SMEM),
            whole,
            pl.BlockSpec(memory_space=pltpu.HBM),
            anywhere,
        ],
        out_specs=[whole] * 2,
        out_shape=[
            jax.ShapeDtypeStruct(held.shape, jnp.float32),
            jax.ShapeDtypeStruct((FREQS, bands.shape[1] + 1, BLOCK), jnp.float32),
        ],
        scratch_shapes=[pltpu.SemaphoreType.DMA],
        cost_estimate=pl.CostEstimate(flops=1 << 18, bytes_accessed=1 << 20, transcendentals=0),
        name="spread_sums",
    )(mask, bands, earlier, held)


def moving_kernel(parts, ids, *refs):
    pieces, (stokes_ref, power_ref, loaded, sems) = refs[: len(parts)], refs[len(parts) :]
    loads, copies = [], []
    for index, (_, _, many) in enumerate(parts):
        loads.append(
            pltpu.make_async_copy(pieces[index], loaded.at[index, pl.ds(0, many)], sems.at[index, 0])
        )
        loads[-1].start()
    for index, (step, start, many) in enumerate(parts):
        span = pl.ds(MINE * ids[2 * SLOTS + step] + start, many)
        loads[index].wait()
        copies.append(
            pltpu.make_async_copy(
                loaded.at[index, pl.ds(0, many)], stokes_ref.at[0, span], sems.at[index, 1]
            )
        )
        copies[-1].start()
        for channel in range(many):
            i_re, i_im = loaded[index, channel, 0, 0], loaded[index, channel, 0, 1]
            power_ref[index, channel] = i_re * i_re + i_im * i_im
    for copy in copies:
        copy.wait()


def place(parts, ids, pieces):
    placed = pl.BlockSpec(memory_space=pltpu.HBM)
    count = len(parts)
    return pl.pallas_call(
        lambda *refs: moving_kernel(parts, *refs),
        in_specs=[pl.BlockSpec(memory_space=pltpu.SMEM)] + [placed] * count,
        out_specs=[placed, pl.BlockSpec(memory_space=pltpu.VMEM)],
        out_shape=[
            jax.ShapeDtypeStruct((1, MINE * SLOTS) + PLANES, jnp.float32),
            jax.ShapeDtypeStruct((count, MINE, BLOCK, BLOCK), jnp.float32),
        ],
        scratch_shapes=[
            pltpu.VMEM((count, MINE) + PLANES, jnp.float32),
            pltpu.SemaphoreType.DMA((count, 2)),
        ],
        compiler_params=pltpu.CompilerParams(vmem_limit_bytes=16 << 20),
        cost_estimate=pl.CostEstimate(
            flops=count << 17, bytes_accessed=count << 21, transcendentals=0
        ),
        name="place",
    )(ids, *pieces)


def bands_of(count_ref, planes_ref, mean_ref, var_ref):
    count = jnp.sum(count_ref[...], axis=0, keepdims=True)
    bands = []
    for band in range(BLOCK // BAND):
        rows = slice(band * BAND, (band + 1) * BAND)
        first = planes_ref[0, rows] / count
        second = planes_ref[1, rows] / count
        mean = mean_ref[0, rows]
        blended = (1.0 - mixing) * mean + mixing * first
        spread = (
            (1.0 - mixing) * var_ref[0, rows]
            + mixing * (second - first * first)
            + mixing * (1.0 - mixing) * (first - mean) ** 2
        )
        bands.append((rows, blended, spread))
    return bands


def weigh_kernel(parts, ids, mask, count_ref, planes_ref, mean_ref, var_ref, *refs):
    power_ref, weight_ref, stage, sems = refs
    copies = []
    bands = bands_of(count_ref, planes_ref, mean_ref, var_ref)
    for index, (step, start, many) in enumerate(parts):
        place = MINE * ids[2 * SLOTS + step] + start
        for channel in range(many):
            live = mask[place + channel].astype(jnp.float32)
            for rows, blended, spread in bands:
                off = power_ref[index, channel, rows] - blended
                stage[index, channel, rows] = live / (1.0 + off * off / spread)
        copies.append(
            pltpu.make_async_copy(
                stage.at[index, pl.ds(0, many)],
                weight_ref.at[0, pl.ds(place, many)],
                sems.at[index],
            )
        )
        copies[-1].start()
    for copy in copies:
        copy.wait()


def weigh(parts, cost, ids, mask, ready, powers):
    whole = pl.BlockSpec(memory_space=pltpu.VMEM)
    scalars = pl.BlockSpec(memory_space=pltpu.SMEM)
    count = len(parts)
    return pl.pallas_call(
        lambda *refs: weigh_kernel(parts, *refs),
        in_specs=[scalars] * 2 + [whole] * 5,
        out_specs=pl.BlockSpec(memory_space=pltpu.HBM),
        out_shape=jax.ShapeDtypeStruct((1, MINE * SLOTS, BLOCK, BLOCK), jnp.float32),
        scratch_shapes=[
            pltpu.VMEM((count, MINE, BLOCK, BLOCK), jnp.float32),
            pltpu.SemaphoreType.DMA((count,)),
        ],
        compiler_params=pltpu.CompilerParams(vmem_limit_bytes=16 << 20),
        cost_estimate=pl.CostEstimate(flops=cost, bytes_accessed=1 << 20, transcendentals=0),
        name="weigh",
    )(ids, mask, *ready, powers)


def finish_kernel(parts, ids, mask, count_ref, planes_ref, mean_ref, var_ref, *refs):
    pieces, (stokes_ref, weight_ref, loaded, stage, sems) = refs[: len(parts)], refs[-5:]
    loads, copies = [], []
    for index, (_, _, many) in enumerate(parts):
        loads.append(
            pltpu.make_async_copy(pieces[index], loaded.at[index, pl.ds(0, many)], sems.at[index, 0])
        )
        loads[-1].start()
    bands = bands_of(count_ref, planes_ref, mean_ref, var_ref)
    for index, (step, start, many) in enumerate(parts):
        place = MINE * ids[2 * SLOTS + step] + start
        span, held = pl.ds(place, many), pl.ds(0, many)
        loads[index].wait()
        copies.append(
            pltpu.make_async_copy(
                loaded.at[index, held], stokes_ref.at[0, span], sems.at[index, 1]
            )
        )
        copies[-1].start()
        for channel in range(many):
            live = mask[place + channel].astype(jnp.float32)
            for rows, blended, spread in bands:
                i_re, i_im = loaded[index, channel, 0, 0, rows], loaded[index, channel, 0, 1, rows]
                off = i_re * i_re + i_im * i_im - blended
                stage[index, channel, rows] = live / (1.0 + off * off / spread)
        copies.append(
            pltpu.make_async_copy(stage.at[index, held], weight_ref.at[0, span], sems.at[index, 2])
        )
        copies[-1].start()
    for copy in copies:
        copy.wait()


def finish(parts, cost, ids, mask, ready, pieces, outs):
    whole = pl.BlockSpec(memory_space=pltpu.VMEM)
    scalars = pl.BlockSpec(memory_space=pltpu.SMEM)
    placed = pl.BlockSpec(memory_space=pltpu.HBM)
    count = len(parts)
    return pl.pallas_call(
        lambda *refs: finish_kernel(parts, *refs),
        in_specs=[scalars] * 2
        + [whole] * 4
        + [placed] * count
        + [placed] * len(outs),
        out_specs=[placed] * 2,
        out_shape=[
            jax.ShapeDtypeStruct((1, MINE * SLOTS) + PLANES, jnp.float32),
            jax.ShapeDtypeStruct((1, MINE * SLOTS, BLOCK, BLOCK), jnp.float32),
        ],
        input_output_aliases={6 + count + index: index for index in range(len(outs))},
        scratch_shapes=[
            pltpu.VMEM((count, MINE) + PLANES, jnp.float32),
            pltpu.VMEM((count, MINE, BLOCK, BLOCK), jnp.float32),
            pltpu.SemaphoreType.DMA((count, 3)),
        ],
        compiler_params=pltpu.CompilerParams(vmem_limit_bytes=16 << 20),
        cost_estimate=pl.CostEstimate(
            flops=cost, bytes_accessed=count << 21, transcendentals=0
        ),
        name=f"finish_{count}",
    )(ids, mask, *ready, *pieces, *outs)


def swap(value, names, size, step):
    return lax.ppermute(value, names, [(i, i ^ step) for i in range(size)])


def exchange(value, names):
    return lax.all_to_all(value, names, split_axis=0, concat_axis=0, tiled=True)


def local(voltages, pattern, owner_map, channel_mask, running_mean, running_var):
    total, _, signals, depth = voltages.shape
    own = lax.axis_index(TM)
    slots = jnp.arange(SLOTS, dtype=jnp.int32)
    order = own ^ slots
    tiles = jnp.sum(jnp.where(order[:, None] == slots[None], owner_map[None], 0), axis=1)
    corners = jnp.sum(jnp.where((tiles[:, None] == slots[None])[..., None], pattern[None], 0), axis=1)
    lives = jnp.sum(
        jnp.where(own == slots[:, None], channel_mask.reshape(SLOTS, MINE), 0), axis=0
    )
    ids = jnp.concatenate([corners[:, 0], corners[:, 1], order, lives]).astype(jnp.int32)

    turned = exchange(voltages, ALL)
    turned = turned.reshape(4, FREQS // 4, SLOTS, MINE, 2, signals, depth)
    crossing, early = correlate((2,), ids, turned, [], depth * SLOTS)
    *held, moments = correlate((0, 1, 3), ids, turned, [early], depth * SLOTS)
    held.insert(2, crossing)
    pieces = held[:1] + [swap(held[number], TM, SLOTS, number) for number in range(1, SLOTS)]

    rows = BLOCK // FREQS
    part = exchange(moments.reshape(FREQS * SLOTS, 2 * rows, BLOCK), ALL)
    last, part = spread_sums(channel_mask, part, pieces[2], held[4])
    parts = exchange(part, FREQ)
    last = swap(last, TM, SLOTS, 3)
    planes = parts[:, : 2 * rows].reshape(FREQS, 2, rows, BLOCK).transpose(1, 0, 2, 3)
    ready = (parts[:, 2 * rows], planes.reshape(2, BLOCK, BLOCK), running_mean, running_var)
    stokes, powers = place(PARTS[:4], ids, pieces)
    weights = weigh(PARTS[:4], 1 << 33, ids, channel_mask, ready, powers)
    return tuple(
        finish(PARTS[4:], 1 << 20, ids, channel_mask, ready, [last], [stokes, weights])
    )


def solution(mesh):
    torus = Mesh(mesh.devices.reshape(SHAPE), ALL)
    return jax.shard_map(
        local,
        mesh=torus,
        in_specs=(
            P(None, None, FREQ, TM),
            P(),
            P(),
            P(FREQ),
            P(TM, None, None),
            P(TM, None, None),
        ),
        out_specs=(P(TM, FREQ, None, None, None, None), P(TM, FREQ, None, None)),
        check_vma=False,
    )
```
